512 devices in a mesh: dp: 4 (over x), ep: 128 (over y, z, core).
Axes of the slice: x: 4, y: 4, z: 16, core: 2. Of those that a mesh axis runs over, the one named last changes fastest.
Arguments:
- hidden_states: bfloat16 [4096, 3584], P(('dp', 'ep')), parts along dimension 0, may hold values from -120 to 120
- norm_gain: float32 [3584], replicated, may hold values from 0.1 to 1.9
- expert_ids: int32 [4096, 8], P(('dp', 'ep')), parts along dimension 0, may hold values from 0 to 15, all different within a row; in each aligned block of 8 rows (0 to 7, 8 to 15, ...) at most 5 rows name the same one
- route_scores: float32 [4096, 8], P(('dp', 'ep')), parts along dimension 0, may hold values from 0.1 to 1
- gate_weight: bfloat16 [3584, 16384], P(None, 'ep'), may hold values from -0.09375 to 0.09375
- up_weight: bfloat16 [3584, 16384], P(None, 'ep'), may hold values from -0.09375 to 0.09375
- down_weight: bfloat16 [16384, 3584], P('ep'), may hold values from -0.1875 to 0.1875
- query_latent: bfloat16 [4096, 64, 512], P(('dp', 'ep')), parts along dimension 0, may hold values from -23 to 23
- query_rope: bfloat16 [4096, 4096], P(('dp', 'ep')), parts along dimension 0, may hold values from -23 to 23
- cache_latent: bfloat16 [512, 512, 512], P(('dp', 'ep')), parts along dimension 0, may hold values from -5.3 to 5.3
- cache_rope: bfloat16 [512, 64, 512], P(('dp', 'ep')), parts along dimension 0, may hold values from -5.3 to 5.3
- tree_latent: bfloat16 [4096, 512], P(('dp', 'ep')), parts along dimension 0, may hold values from -6 to 6
- tree_rope: bfloat16 [4096, 64], P(('dp', 'ep')), parts along dimension 0, may hold values from -6 to 6
- cache_lengths: int32 [512], P(('dp', 'ep')), parts along dimension 0, may hold values from 128 to 512, as said below
- tree_parents: int32 [4096], P(('dp', 'ep')), parts along dimension 0, may hold values from 0 to 6, as said below
Outputs:
- attention_out: bfloat16 [4096, 64, 512], P(('dp', 'ep')), parts along dimension 0
- expert_out: bfloat16 [4096, 3584], P(('dp', 'ep')), parts along dimension 0
The draws below stay inside these ranges and needn't reach their ends.
There are 4 independent parts, one for each index of `dp`. The reference program is written for one: setup_inputs(seed, part) draws one part's arguments, and reference() takes and returns one part's arrays. A program takes and returns all parts, laid end to end along the dimension named above; an argument that names none is the same for every part. Nothing has to cross between parts.
Inputs may be any that keep to these rules, and one draw needn't show every extreme that they name: `expert_ids`: in the 8 rows of one device each expert is named by at most 5 rows, a bound that some block reaches; each row names 8 different experts. `cache_lengths`: some request holds exactly 512 positions. `tree_parents`: counting candidates from 0 within their request, candidate i > 0 has a parent below i, and candidate 0 has 0.
All inputs are finite; a program needn't handle non-finite values.
Results may differ from the reference program's by a relative error of at most 0.008.
Values may be sent and summed in bfloat16 or wider, within the bound.
No kernel may reach another device: no remote copies, remote signals or barrier semaphores. Data moves between devices by JAX's collectives and lax.ppermute only.
A program may use at most 64 MiB of HBM per device.

```python
import math
import jax
import jax.numpy as jnp
import numpy as np
from jax import lax

D = 3584
HID = 1024
EXPERTS = 16
TOP = 8
MOST = 5
H = 64
LAT = 512
ROPE = 64
ROWS_DEV = 8
CACHE = 512
REQS = 128
ROWS = 1024


def cache_parts(key):
    latent = jnp.clip(jax.random.normal(jax.random.fold_in(key, 101), (REQS, CACHE, LAT), jnp.float32), -4.0, 4.0)
    rotary = jnp.clip(jax.random.normal(jax.random.fold_in(key, 102), (REQS, CACHE, ROPE), jnp.float32), -4.0, 4.0)
    return (latent, rotary)


def query_parts(key):
    base_latent = jnp.clip(jax.random.normal(jax.random.fold_in(key, 201), (ROWS, H, LAT), jnp.float32), -4.0, 4.0)
    base_rotary = jnp.clip(jax.random.normal(jax.random.fold_in(key, 202), (ROWS, H, ROPE), jnp.float32), -4.0, 4.0)
    return (base_latent, base_rotary.reshape(ROWS, H * ROPE))


def draw_cache_latent(key, part):
    return cache_parts(key)[0].astype(jnp.bfloat16)


def draw_cache_rope(key, part):
    return jnp.transpose(cache_parts(key)[1], (0, 2, 1)).astype(jnp.bfloat16)


def draw_query_latent(key, part):
    return query_parts(key)[0].astype(jnp.bfloat16)


def draw_query_rope(key, part):
    return query_parts(key)[1].astype(jnp.bfloat16)


def draw_hidden_states(key, part):
    base = jnp.clip(jax.random.normal(jax.random.fold_in(key, 402), (ROWS, D), jnp.float32), -4.0, 4.0)
    per_row_scale = jnp.exp(jax.random.uniform(jax.random.fold_in(key, 403), (ROWS, 1), jnp.float32, jnp.log(0.3), jnp.log(3.0)))
    column_scale = jnp.exp(jax.random.uniform(jax.random.fold_in(key, 404), (1, D), jnp.float32, 0.0, jnp.log(10.0)))
    return (base * per_row_scale * column_scale).astype(jnp.bfloat16)


def draw_cache_lengths(key, part):
    raw = jax.random.randint(jax.random.fold_in(key, 301), (REQS,), CACHE // 4, CACHE + 1)
    chosen = jax.random.randint(jax.random.fold_in(key, 302), (), 0, REQS)
    return jnp.where(jnp.arange(REQS) == chosen, CACHE, raw).astype(jnp.int32)


def draw_tree_parents(key, part):
    raw = jax.random.randint(jax.random.fold_in(key, 501), (REQS, ROWS_DEV), 0, 1048576)
    position = jnp.arange(ROWS_DEV, dtype=jnp.int32)[None, :]
    return (raw % jnp.maximum(position, 1)).reshape(ROWS).astype(jnp.int32)


def block_scale(key, shape, split, least, high):
    factor_of, own = 1.0, jax.random.fold_in(key, 6)
    for dim, shards_of in split:
        draws = jnp.exp(jax.random.uniform(jax.random.fold_in(own, dim), (shards_of,), jnp.float32, least / len(split), high / len(split)))
        factor_of = factor_of * jnp.repeat(draws, shape[dim] // shards_of).reshape([-1 if axis == dim else 1 for axis in range(len(shape))])
    return factor_of


def routed_block(stream_key, own, number, rows, count, top, reach, slope):
    order = jax.random.permutation(stream_key, count)
    heavy_load, common = portions_of(count, rows * top, reach, slope, True), portions_of(count, rows * top, reach, slope, False)
    places = jnp.arange(count)

    def named(sizes, turn):
        used = int((sizes > 0).sum())
        fixed = max(1, used // 4)
        passed = fixed + (places - fixed + turn * (used - fixed)) % max(1, count - fixed)
        return jnp.zeros((count,), jnp.int32).at[order[jnp.where(places < fixed, places, passed)]].set(jnp.asarray(sizes, jnp.int32))

    sizes = jnp.where(number % 4 == 0, named(heavy_load, number // 4), named(common, number - number // 4 - 1))
    mixed = jax.random.permutation(jax.random.fold_in(own, 3), count)
    donor, sink = mixed[0:count // 2 * 2:2], mixed[1:count // 2 * 2:2]
    room = jnp.minimum(sizes[donor] - 1, reach - sizes[sink]) // 2
    room = jnp.where((donor == order[0]) | (sink == order[0]) | (sizes[sink] == 0), 0, jnp.maximum(room, 0))
    passed = jax.random.randint(jax.random.fold_in(own, 4), (count // 2,), 0, 1 << 20) % (room + 1)
    sizes = sizes.at[donor].add(-passed).at[sink].add(passed)
    items = jnp.searchsorted(jnp.cumsum(sizes), jnp.arange(rows * top), side="right").astype(jnp.int32)
    listing = items.reshape(top, rows).T
    listing = listing[jax.random.permutation(jax.random.fold_in(own, 1), rows)]
    turn = jax.random.randint(jax.random.fold_in(own, 2), (rows, 1), 0, top)
    return jnp.take_along_axis(listing, (jnp.arange(top)[None, :] + turn) % top, axis=1)


def portions_of(count, total, reach, skew, full):
    loads = [(1 << 20) // math.isqrt(standing ** skew) + 1 for standing in range(1, count + 1)]
    largest = reach if full else min(reach, max(-(-total // count), total * loads[0] // sum(loads)))
    least = 1 if total - largest >= count - 1 else 0
    counts, surplus = [largest] + [least] * (count - 1), total - largest - least * (count - 1)
    while surplus > 0:
        free = [i for i in range(1, count) if counts[i] < largest] or [i for i in range(1, count) if counts[i] < reach]
        pool, budget = sum([loads[i] for i in free]), surplus
        for i in free:
            more = min(reach - counts[i], max(1, budget * loads[i] // pool), surplus)
            counts[i] = counts[i] + more
            surplus = surplus - more
    return np.array(counts)


def normal_values(own_key, shape, spread, bound, cuts=(), kind=jnp.bfloat16):
    array = spread * jax.random.normal(own_key, shape, jnp.float32)
    if cuts:
        array = array * block_scale(own_key, shape, cuts, -0.22, 0.18)
    return jnp.clip(array, -bound, bound).astype(kind)


def setup_inputs(seed: int = 0, part: int = 0) -> dict:
    seeds = jax.random.split(jax.random.key(seed), 16)
    part_splits = jax.random.split(jax.random.fold_in(seeds[15], part), 16)
    hidden_states = draw_hidden_states(jax.random.fold_in(jax.random.fold_in(seeds[15], part), 71), part)
    norm_gain = jnp.clip(1.0 + 0.18 * jax.random.normal(seeds[1], (D,), jnp.float32), 0.1, 1.9)
    expert_ids_keys = jax.random.split(jax.random.fold_in(part_splits[2], 1), ROWS // ROWS_DEV)
    expert_ids_turns = jax.random.permutation(jax.random.fold_in(part_splits[2], 3), ROWS // ROWS_DEV)
    expert_ids = jax.vmap(lambda own, number: routed_block(jax.random.fold_in(part_splits[2], 2), own, number, ROWS_DEV, EXPERTS, TOP, MOST, 2))(expert_ids_keys, expert_ids_turns).reshape((ROWS, TOP))
    route_scores = jnp.clip(jnp.exp(math.log(1.0) - 2.3025851 * jax.random.uniform(part_splits[3], (ROWS, TOP), jnp.float32) ** block_scale(part_splits[3], (ROWS, TOP), ((0, 128),), -0.2, 0.2)), 0.1, 1.0)
    gate_weight = normal_values(seeds[4], (D, EXPERTS * HID), D ** -0.5, 0.09375, ((1, 128),))
    up_weight = normal_values(seeds[5], (D, EXPERTS * HID), D ** -0.5, 0.09375, ((1, 128),))
    down_weight = normal_values(seeds[6], (EXPERTS * HID, D), HID ** -0.5, 0.1875, ((0, 128),))
    query_latent = draw_query_latent(jax.random.fold_in(jax.random.fold_in(seeds[15], part), 71), part)
    query_rope = draw_query_rope(jax.random.fold_in(jax.random.fold_in(seeds[15], part), 71), part)
    cache_latent = draw_cache_latent(jax.random.fold_in(jax.random.fold_in(seeds[15], part), 71), part)
    cache_rope = draw_cache_rope(jax.random.fold_in(jax.random.fold_in(seeds[15], part), 71), part)
    tree_latent = normal_values(part_splits[11], (ROWS, LAT), 1.5, 6.0, ((0, 128),))
    tree_rope = normal_values(part_splits[12], (ROWS, ROPE), 1.5, 6.0, ((0, 128),))
    cache_lengths = draw_cache_lengths(jax.random.fold_in(jax.random.fold_in(seeds[15], part), 71), part)
    tree_parents = draw_tree_parents(jax.random.fold_in(jax.random.fold_in(seeds[15], part), 71), part)
    return {"hidden_states": hidden_states, "norm_gain": norm_gain, "expert_ids": expert_ids, "route_scores": route_scores, "gate_weight": gate_weight, "up_weight": up_weight, "down_weight": down_weight, "query_latent": query_latent, "query_rope": query_rope, "cache_latent": cache_latent, "cache_rope": cache_rope, "tree_latent": tree_latent, "tree_rope": tree_rope, "cache_lengths": cache_lengths, "tree_parents": tree_parents}


softmax_scale = 192.0 ** (-0.5)
route_scale = 2.5
norm_eps = 1e-06
very_negative = -1e+30

def visible_tree(parents):
    tree_size = parents.shape[0]
    position = jnp.arange(tree_size, dtype=jnp.int32)
    parent_map = ((parents[:, None] == position[None, :]) & (position[:, None] > 0)).astype(jnp.float32)
    identity = jnp.eye(tree_size, dtype=jnp.float32)
    reached = identity
    for sweep_index in range(tree_size):
        reached = jnp.minimum(identity + jnp.dot(parent_map, reached, precision=lax.Precision.HIGHEST), 1.0)
    return reached > 0.5

def attend_request(operands):
    query_latent, query_rope, cache_latent, cache_rope, tree_latent, tree_rope, cache_length, parents = operands
    row_count = query_latent.shape[0]
    head_count = query_latent.shape[1]
    rope_width = tree_rope.shape[1]
    query_lat32 = query_latent.astype(jnp.float32)
    query_rot32 = query_rope.reshape(row_count, head_count, rope_width).astype(jnp.float32)
    cache_lat32 = cache_latent.astype(jnp.float32)
    tree_lat32 = tree_latent.astype(jnp.float32)
    cache_scores = jnp.einsum('rhc,lc->rhl', query_lat32, cache_lat32)
    cache_scores = (cache_scores + jnp.einsum('rhc,cl->rhl', query_rot32, cache_rope.astype(jnp.float32))) * softmax_scale
    candidate_tree_scores = jnp.einsum('rhc,jc->rhj', query_lat32, tree_lat32)
    candidate_tree_scores = (candidate_tree_scores + jnp.einsum('rhc,jc->rhj', query_rot32, tree_rope.astype(jnp.float32))) * softmax_scale
    cache_live = (jnp.arange(cache_latent.shape[0], dtype=jnp.int32) < cache_length)[None, None, :]
    tree_seen = visible_tree(parents)[:, None, :]
    cache_scores = jnp.where(cache_live, cache_scores, very_negative)
    candidate_tree_scores = jnp.where(tree_seen, candidate_tree_scores, very_negative)
    row_peak = jnp.maximum(lax.optimization_barrier(jnp.max(cache_scores, axis=-1, keepdims=True)), lax.optimization_barrier(jnp.max(candidate_tree_scores, axis=-1, keepdims=True)))
    cache_exp = jnp.where(cache_live, jnp.exp(cache_scores - row_peak), 0.0)
    tree_exp = jnp.where(tree_seen, jnp.exp(candidate_tree_scores - row_peak), 0.0)
    denominator = lax.optimization_barrier(jnp.sum(cache_exp, axis=-1, keepdims=True)) + lax.optimization_barrier(jnp.sum(tree_exp, axis=-1, keepdims=True))
    cache_probs = (cache_exp / denominator).astype(jnp.bfloat16).astype(jnp.float32)
    tree_probs = (tree_exp / denominator).astype(jnp.bfloat16).astype(jnp.float32)
    attended = jnp.einsum('rhl,lc->rhc', cache_probs, cache_lat32) + jnp.einsum('rhj,jc->rhc', tree_probs, tree_lat32)
    return attended.astype(jnp.bfloat16)

def reference(hidden_states, norm_gain, expert_ids, route_scores, gate_weight, up_weight, down_weight, query_latent, query_rope, cache_latent, cache_rope, tree_latent, tree_rope, cache_lengths, tree_parents):
    attention_out = lax.map(attend_request, (query_latent.reshape(REQS, ROWS_DEV, H, LAT), query_rope.reshape(REQS, ROWS_DEV, H * ROPE), cache_latent, cache_rope, tree_latent.reshape(REQS, ROWS_DEV, LAT), tree_rope.reshape(REQS, ROWS_DEV, ROPE), cache_lengths, tree_parents.reshape(REQS, ROWS_DEV))).reshape(ROWS, H, LAT)
    states = hidden_states.astype(jnp.float32)
    normed = (states * lax.rsqrt(lax.optimization_barrier(jnp.mean(states * states, axis=-1, keepdims=True)) + norm_eps) * norm_gain).astype(jnp.bfloat16)
    router_weight_matrix = (route_scale * route_scores / lax.optimization_barrier(jnp.sum(route_scores, axis=-1, keepdims=True))).astype(jnp.bfloat16)
    matches = expert_ids[:, :, None] == jnp.arange(EXPERTS, dtype=jnp.int32)[None, None, :]
    merge_expert_outputs = lax.optimization_barrier(jnp.sum(jnp.where(matches, router_weight_matrix.astype(jnp.float32)[:, :, None], 0.0), axis=1)).astype(jnp.bfloat16)

    def expert_step(running, expert_index):
        start = (expert_index * HID).astype(jnp.int32)
        gate_cols = lax.dynamic_slice_in_dim(gate_weight, start, HID, 1)
        up_cols = lax.dynamic_slice_in_dim(up_weight, start, HID, 1)
        down_rows = lax.dynamic_slice_in_dim(down_weight, start, HID, 0)
        gate_act = jnp.dot(normed, gate_cols, preferred_element_type=jnp.float32)
        up_act = jnp.dot(normed, up_cols, preferred_element_type=jnp.float32)
        share = lax.dynamic_slice_in_dim(merge_expert_outputs, expert_index, 1, 1).astype(jnp.float32)
        expert_hidden = (share * jax.nn.silu(gate_act) * up_act).astype(jnp.bfloat16)
        return (running + jnp.dot(expert_hidden, down_rows, preferred_element_type=jnp.float32), None)
    summed, unused = lax.scan(expert_step, jnp.zeros((ROWS, D), jnp.float32), jnp.arange(EXPERTS, dtype=jnp.int32))
    return (attention_out, summed.astype(jnp.bfloat16))
```

```python
import jax
import jax.numpy as jnp
from jax import lax
from jax.sharding import Mesh, PartitionSpec as P

HID = 1024
EXPERTS = 16

softmax_scale = 192.0 ** (-0.5)
route_scale = 2.5
norm_eps = 1e-06
very_negative = -1e30
grid_axes = ("dp", "y", "z", "c")


def visible_tree(parents):
    tree_size = parents.shape[0]
    position = jnp.arange(tree_size, dtype=jnp.int32)
    parent_map = ((parents[:, None] == position[None, :]) & (position[:, None] > 0)).astype(
        jnp.float32
    )
    identity = jnp.eye(tree_size, dtype=jnp.float32)
    reached = identity
    for sweep_index in range(tree_size):
        reached = jnp.minimum(
            identity + jnp.dot(parent_map, reached, precision=lax.Precision.HIGHEST), 1.0
        )
    return reached > 0.5


def attend_request(
    query_latent,
    query_rope,
    cache_latent,
    cache_rope,
    tree_latent,
    tree_rope,
    cache_length,
    parents,
):
    row_count = query_latent.shape[0]
    head_count = query_latent.shape[1]
    rope_width = tree_rope.shape[1]
    query_rotary = query_rope.reshape(row_count, head_count, rope_width)
    cache_scores = jnp.einsum(
        "rhc,lc->rhl", query_latent, cache_latent, preferred_element_type=jnp.float32
    )
    cache_scores = (
        cache_scores
        + jnp.einsum("rhc,cl->rhl", query_rotary, cache_rope, preferred_element_type=jnp.float32)
    ) * softmax_scale
    candidate_tree_scores = jnp.einsum(
        "rhc,jc->rhj", query_latent, tree_latent, preferred_element_type=jnp.float32
    )
    candidate_tree_scores = (
        candidate_tree_scores
        + jnp.einsum("rhc,jc->rhj", query_rotary, tree_rope, preferred_element_type=jnp.float32)
    ) * softmax_scale
    cache_live = (jnp.arange(cache_latent.shape[0], dtype=jnp.int32) < cache_length)[None, None, :]
    tree_seen = visible_tree(parents)[:, None, :]
    cache_scores = jnp.where(cache_live, cache_scores, very_negative)
    candidate_tree_scores = jnp.where(tree_seen, candidate_tree_scores, very_negative)
    row_peak = jnp.maximum(
        jnp.max(cache_scores, axis=-1, keepdims=True),
        jnp.max(candidate_tree_scores, axis=-1, keepdims=True),
    )
    cache_exp = jnp.where(cache_live, jnp.exp(cache_scores - row_peak), 0.0)
    tree_exp = jnp.where(tree_seen, jnp.exp(candidate_tree_scores - row_peak), 0.0)
    denominator = jnp.sum(cache_exp, axis=-1, keepdims=True) + jnp.sum(
        tree_exp, axis=-1, keepdims=True
    )
    cache_probs = (cache_exp / denominator).astype(jnp.bfloat16)
    tree_probs = (tree_exp / denominator).astype(jnp.bfloat16)
    attended = jnp.einsum(
        "rhl,lc->rhc", cache_probs, cache_latent, preferred_element_type=jnp.float32
    )
    attended = attended + jnp.einsum(
        "rhj,jc->rhc", tree_probs, tree_latent, preferred_element_type=jnp.float32
    )
    return attended.astype(jnp.bfloat16)


def combine_table(expert_ids, route_scores):
    router_weight_matrix = (
        route_scale * route_scores / jnp.sum(route_scores, axis=-1, keepdims=True)
    ).astype(jnp.bfloat16)
    matches = expert_ids[:, :, None] == jnp.arange(EXPERTS, dtype=jnp.int32)[None, None, :]
    return jnp.sum(
        jnp.where(matches, router_weight_matrix.astype(jnp.float32)[:, :, None], 0.0), axis=1
    ).astype(jnp.bfloat16)


def swap_core(value):
    return lax.ppermute(value, "c", [(0, 1), (1, 0)])


def gated(rows, share, gate_weight, up_weight, down_weight):
    gate_act = jnp.dot(rows, gate_weight, preferred_element_type=jnp.float32)
    up_act = jnp.dot(rows, up_weight, preferred_element_type=jnp.float32)
    hidden = (share * jax.nn.silu(gate_act) * up_act).astype(jnp.bfloat16)
    return jnp.dot(hidden, down_weight, preferred_element_type=jnp.float32)


def local(
    hidden_states,
    norm_gain,
    expert_ids,
    route_scores,
    gate_weight,
    up_weight,
    down_weight,
    query_latent,
    query_rope,
    cache_latent,
    cache_rope,
    tree_latent,
    tree_rope,
    cache_lengths,
    tree_parents,
):
    other = [swap_core(w) for w in (gate_weight, up_weight, down_weight)]
    states = hidden_states.astype(jnp.float32)
    normed = (
        states * lax.rsqrt(jnp.mean(states * states, axis=-1, keepdims=True) + norm_eps) * norm_gain
    ).astype(jnp.bfloat16)
    width = normed.shape[1]
    combine = combine_table(expert_ids, route_scores)
    packed = jnp.concatenate(
        [normed, jnp.pad(combine, ((0, 0), (0, 128 - EXPERTS)))], axis=1
    )
    gathered = lax.all_gather(packed, ("y", "z"), axis=0, tiled=True)

    attention_out = attend_request(
        query_latent,
        query_rope,
        cache_latent[0],
        cache_rope[0],
        tree_latent,
        tree_rope,
        cache_lengths[0],
        tree_parents,
    )

    chip = lax.axis_index("y") * lax.axis_size("z") + lax.axis_index("z")
    unit_count = 2 * gate_weight.shape[1]
    expert = chip * unit_count // HID
    rows = gathered[:, :width]
    shares = gathered[:, width:].astype(jnp.float32)
    share = jnp.sum(
        jnp.where(jnp.arange(shares.shape[1])[None, :] == expert, shares, 0.0),
        axis=1,
        keepdims=True,
    )
    partial = gated(rows, share, gate_weight, up_weight, down_weight) + gated(rows, share, *other)
    expert_out = lax.psum_scatter(
        partial.astype(jnp.bfloat16), ("y", "z"), scatter_dimension=0, tiled=True
    )
    return (attention_out, expert_out)


def solution(mesh):
    devices = mesh.devices.reshape(4, 4, 16, 2)
    grid = Mesh(devices, grid_axes)
    rows = P(grid_axes, None)
    ep = ("y", "z", "c")
    placed = (
        rows,
        P(),
        rows,
        rows,
        P(None, ep),
        P(None, ep),
        P(ep, None),
        P(grid_axes, None, None),
        rows,
        P(grid_axes, None, None),
        P(grid_axes, None, None),
        rows,
        rows,
        P(grid_axes),
        P(grid_axes),
    )
    return jax.shard_map(
        local,
        mesh=grid,
        in_specs=placed,
        out_specs=(P(grid_axes, None, None), rows),
        check_vma=False,
    )
```

```python
import jax
import jax.numpy as jnp
from jax import lax
from jax.experimental import pallas as pl
from jax.experimental.pallas import tpu as pltpu
from jax.sharding import Mesh, PartitionSpec as P

HID = 1024
EXPERTS = 16
MOST = 5

softmax_scale = 192.0 ** (-0.5)
route_scale = 2.5
norm_eps = 1e-06
very_negative = -1e30
grid_axes = ("dp", "y", "z", "c")


def visible_tree(parents):
    tree_size = parents.shape[0]
    position = jnp.arange(tree_size, dtype=jnp.int32)
    parent_map = ((parents[:, None] == position[None, :]) & (position[:, None] > 0)).astype(
        jnp.float32
    )
    identity = jnp.eye(tree_size, dtype=jnp.float32)
    reached = identity
    for sweep_index in range(tree_size):
        reached = jnp.minimum(
            identity + jnp.dot(parent_map, reached, precision=lax.Precision.HIGHEST), 1.0
        )
    return reached > 0.5


def attend_request(
    query_latent,
    query_rope,
    cache_latent,
    cache_rope,
    tree_latent,
    tree_rope,
    cache_length,
    parents,
):
    row_count = query_latent.shape[0]
    head_count = query_latent.shape[1]
    rope_width = tree_rope.shape[1]
    query_rotary = query_rope.reshape(row_count, head_count, rope_width)
    cache_scores = jnp.einsum(
        "rhc,lc->rhl", query_latent, cache_latent, preferred_element_type=jnp.float32
    )
    cache_scores = (
        cache_scores
        + jnp.einsum("rhc,cl->rhl", query_rotary, cache_rope, preferred_element_type=jnp.float32)
    ) * softmax_scale
    candidate_tree_scores = jnp.einsum(
        "rhc,jc->rhj", query_latent, tree_latent, preferred_element_type=jnp.float32
    )
    candidate_tree_scores = (
        candidate_tree_scores
        + jnp.einsum("rhc,jc->rhj", query_rotary, tree_rope, preferred_element_type=jnp.float32)
    ) * softmax_scale
    cache_live = (jnp.arange(cache_latent.shape[0], dtype=jnp.int32) < cache_length)[None, None, :]
    tree_seen = visible_tree(parents)[:, None, :]
    cache_scores = jnp.where(cache_live, cache_scores, very_negative)
    candidate_tree_scores = jnp.where(tree_seen, candidate_tree_scores, very_negative)
    row_peak = jnp.maximum(
        jnp.max(cache_scores, axis=-1, keepdims=True),
        jnp.max(candidate_tree_scores, axis=-1, keepdims=True),
    )
    cache_exp = jnp.where(cache_live, jnp.exp(cache_scores - row_peak), 0.0)
    tree_exp = jnp.where(tree_seen, jnp.exp(candidate_tree_scores - row_peak), 0.0)
    denominator = jnp.sum(cache_exp, axis=-1, keepdims=True) + jnp.sum(
        tree_exp, axis=-1, keepdims=True
    )
    cache_probs = (cache_exp / denominator).astype(jnp.bfloat16)
    tree_probs = (tree_exp / denominator).astype(jnp.bfloat16)
    attended = jnp.einsum(
        "rhl,lc->rhc", cache_probs, cache_latent, preferred_element_type=jnp.float32
    )
    attended = attended + jnp.einsum(
        "rhj,jc->rhc", tree_probs, tree_latent, preferred_element_type=jnp.float32
    )
    return attended.astype(jnp.bfloat16)


def combine_table(expert_ids, route_scores):
    router_weight_matrix = (
        route_scale * route_scores / jnp.sum(route_scores, axis=-1, keepdims=True)
    ).astype(jnp.bfloat16)
    matches = expert_ids[:, :, None] == jnp.arange(EXPERTS, dtype=jnp.int32)[None, None, :]
    return jnp.sum(
        jnp.where(matches, router_weight_matrix.astype(jnp.float32)[:, :, None], 0.0), axis=1
    ).astype(jnp.bfloat16)


def shifted(value, axis, step):
    size = lax.axis_size(axis)
    return lax.ppermute(value, axis, [(i, (i + step) % size) for i in range(size)])


def expert_body(rows, gate_a, up_a, down_a, gate_b, up_b, down_b, out):
    value = rows[...]

    def hidden(gate, up):
        gate_act = jnp.dot(value, gate[...], preferred_element_type=jnp.float32)
        up_act = jnp.dot(value, up[...], preferred_element_type=jnp.float32)
        return (gate_act / (1.0 + jnp.exp(-gate_act)) * up_act).astype(jnp.bfloat16)

    total = jnp.dot(hidden(gate_a, up_a), down_a[...], preferred_element_type=jnp.float32)
    total += jnp.dot(hidden(gate_b, up_b), down_b[...], preferred_element_type=jnp.float32)
    out[...] = total.astype(jnp.bfloat16)


def expert_part(rows, weights):
    whole = pl.BlockSpec(memory_space=pltpu.VMEM)
    units = 2 * weights[0].shape[1]
    return pl.pallas_call(
        expert_body,
        out_shape=jax.ShapeDtypeStruct(rows.shape, jnp.bfloat16),
        in_specs=[whole] * 7,
        out_specs=whole,
        cost_estimate=pl.CostEstimate(
            flops=6 * rows.shape[0] * rows.shape[1] * units,
            transcendentals=rows.shape[0] * units,
            bytes_accessed=4 * rows.size + 6 * rows.shape[1] * units,
        ),
        compiler_params=pltpu.CompilerParams(vmem_limit_bytes=40 << 20),
    )(rows, *weights)


def local(
    hidden_states,
    norm_gain,
    expert_ids,
    route_scores,
    gate_weight,
    up_weight,
    down_weight,
    query_latent,
    query_rope,
    cache_latent,
    cache_rope,
    tree_latent,
    tree_rope,
    cache_lengths,
    tree_parents,
):
    states = hidden_states.astype(jnp.float32)
    normed = (
        states * lax.rsqrt(jnp.mean(states * states, axis=-1, keepdims=True) + norm_eps) * norm_gain
    ).astype(jnp.bfloat16)
    row_count, width = normed.shape
    combine = combine_table(expert_ids, route_scores)
    packed = jnp.concatenate(
        [normed, jnp.pad(combine, ((0, 0), (0, 128 - EXPERTS)))], axis=1
    )
    gathered = lax.all_gather(packed, "z", axis=0, tiled=True)
    gathered, gate_weight, up_weight, down_weight = lax.optimization_barrier(
        (gathered, gate_weight, up_weight, down_weight)
    )
    own = (gate_weight, up_weight, down_weight)
    weights = own + tuple(shifted(w, "c", 1) for w in own)

    count = gathered.shape[0]
    y_size = lax.axis_size("y")
    per_y = EXPERTS // y_size
    sources = jnp.arange(count, dtype=jnp.int32)
    table = gathered[:, width:]
    to = (lax.axis_index("y") + jnp.arange(y_size, dtype=jnp.int32)) % y_size
    expert = to * per_y + lax.axis_index("z") * per_y // lax.axis_size("z")
    column = (expert[:, None] == jnp.arange(table.shape[1], dtype=jnp.int32)[None, :]).astype(
        jnp.bfloat16
    )
    share = lax.dot_general(
        column, table, (((1,), (1,)), ((), ())), preferred_element_type=jnp.float32
    )
    named = share > 0
    block = sources // row_count
    earlier = (sources[:, None] < sources[None, :]) & (block[:, None] == block[None, :])
    slot = jnp.dot(
        named.astype(jnp.bfloat16), earlier.astype(jnp.bfloat16), preferred_element_type=jnp.float32
    ).astype(jnp.int32)
    slots = count // row_count * MOST
    target = jnp.where(named, block[None, :] * MOST + slot, -1)
    placed = jnp.arange(slots, dtype=jnp.int32)[None, :, None] == target[:, None, :]
    pick = placed.astype(jnp.bfloat16)
    weigh = jnp.where(placed, share[:, None, :], 0.0).astype(jnp.bfloat16)

    rows = gathered[:, :width]
    chosen = [
        jnp.dot(pick[k], rows, preferred_element_type=jnp.float32).astype(jnp.bfloat16)
        for k in range(y_size)
    ]
    returned = []
    for k in range(y_size):
        arrived = shifted(chosen[k], "y", k) if k else chosen[k]
        answer = expert_part(arrived, weights)
        returned.append(shifted(answer, "y", -k) if k else answer)

    attention_out = attend_request(
        query_latent,
        query_rope,
        cache_latent[0],
        cache_rope[0],
        tree_latent,
        tree_rope,
        cache_lengths[0],
        tree_parents,
    )

    summed = sum(
        lax.dot_general(
            weigh[k], returned[k], (((0,), (0,)), ((), ())), preferred_element_type=jnp.float32
        )
        for k in range(y_size)
    ).astype(jnp.bfloat16)
    parts = lax.all_to_all(summed, "z", split_axis=0, concat_axis=0, tiled=True)
    expert_out = jnp.sum(parts.reshape(-1, row_count, width).astype(jnp.float32), axis=0)
    return (attention_out, expert_out.astype(jnp.bfloat16))


def solution(mesh):
    devices = mesh.devices.reshape(4, 4, 16, 2)
    grid = Mesh(devices, grid_axes)
    rows = P(grid_axes, None)
    ep = ("y", "z", "c")
    placed = (
        rows,
        P(),
        rows,
        rows,
        P(None, ep),
        P(None, ep),
        P(ep, None),
        P(grid_axes, None, None),
        rows,
        P(grid_axes, None, None),
        P(grid_axes, None, None),
        rows,
        rows,
        P(grid_axes),
        P(grid_axes),
    )
    return jax.shard_map(
        local,
        mesh=grid,
        in_specs=placed,
        out_specs=(P(grid_axes, None, None), rows),
        check_vma=False,
    )
```

```python
import functools

import jax
import jax.numpy as jnp
from jax import lax
from jax.experimental import pallas as pl
from jax.experimental.pallas import tpu as pltpu
from jax.sharding import Mesh, PartitionSpec as P


EXPERTS = 16
MOST = 5
LANES = 128

softmax_scale = 192.0 ** (-0.5)
route_scale = 2.5
norm_eps = 1e-06
very_negative = -1e30
grid_axes = ("dp", "y", "z", "c")


def visible_tree(parents):
    tree_size = parents.shape[0]
    position = jnp.arange(tree_size, dtype=jnp.int32)
    parent_map = ((parents[:, None] == position[None, :]) & (position[:, None] > 0)).astype(
        jnp.float32
    )
    identity = jnp.eye(tree_size, dtype=jnp.float32)
    reached = identity
    for _ in range(tree_size):
        reached = jnp.minimum(
            identity + jnp.dot(parent_map, reached, precision=lax.Precision.HIGHEST), 1.0
        )
    return reached > 0.5


def attend_request(
    query_latent,
    query_rope,
    cache_latent,
    cache_rope,
    tree_latent,
    tree_rope,
    cache_length,
    parents,
):
    row_count = query_latent.shape[0]
    head_count = query_latent.shape[1]
    rope_width = tree_rope.shape[1]
    query_rotary = query_rope.reshape(row_count, head_count, rope_width)
    cache_scores = jnp.einsum(
        "rhc,lc->rhl", query_latent, cache_latent, preferred_element_type=jnp.float32
    )
    cache_scores = (
        cache_scores
        + jnp.einsum("rhc,cl->rhl", query_rotary, cache_rope, preferred_element_type=jnp.float32)
    ) * softmax_scale
    candidate_tree_scores = jnp.einsum(
        "rhc,jc->rhj", query_latent, tree_latent, preferred_element_type=jnp.float32
    )
    candidate_tree_scores = (
        candidate_tree_scores
        + jnp.einsum("rhc,jc->rhj", query_rotary, tree_rope, preferred_element_type=jnp.float32)
    ) * softmax_scale
    cache_live = (jnp.arange(cache_latent.shape[0], dtype=jnp.int32) < cache_length)[None, None, :]
    tree_seen = visible_tree(parents)[:, None, :]
    cache_scores = jnp.where(cache_live, cache_scores, very_negative)
    candidate_tree_scores = jnp.where(tree_seen, candidate_tree_scores, very_negative)
    row_peak = jnp.maximum(
        jnp.max(cache_scores, axis=-1, keepdims=True),
        jnp.max(candidate_tree_scores, axis=-1, keepdims=True),
    )
    cache_exp = jnp.where(cache_live, jnp.exp(cache_scores - row_peak), 0.0)
    tree_exp = jnp.where(tree_seen, jnp.exp(candidate_tree_scores - row_peak), 0.0)
    denominator = jnp.sum(cache_exp, axis=-1, keepdims=True) + jnp.sum(
        tree_exp, axis=-1, keepdims=True
    )
    cache_probs = (cache_exp / denominator).astype(jnp.bfloat16)
    tree_probs = (tree_exp / denominator).astype(jnp.bfloat16)
    attended = jnp.einsum(
        "rhl,lc->rhc", cache_probs, cache_latent, preferred_element_type=jnp.float32
    )
    attended = attended + jnp.einsum(
        "rhj,jc->rhc", tree_probs, tree_latent, preferred_element_type=jnp.float32
    )
    return attended.astype(jnp.bfloat16)


def pack_body(states, gain, ids, scores, out):
    value = states[...].astype(jnp.float32)
    row_count, width = value.shape
    mean = jnp.mean(value * value, axis=-1, keepdims=True)
    out[:, :width] = (value * lax.rsqrt(mean + norm_eps) * gain[...]).astype(jnp.bfloat16)
    score = scores[...]
    weight = (route_scale * score / jnp.sum(score, axis=-1, keepdims=True)).astype(jnp.bfloat16)
    weight = weight.astype(jnp.float32)
    names = ids[...]
    lane = lax.broadcasted_iota(jnp.int32, (row_count, LANES), 1)
    table = jnp.zeros((row_count, LANES), jnp.float32)
    for k in range(names.shape[1]):
        table += jnp.where(names[:, k : k + 1] == lane, weight[:, k : k + 1], 0.0)
    out[:, width:] = table.astype(jnp.bfloat16)


def select_body(row_count, gathered, *outs):
    chosen, weigh = outs[:-1], outs[-1]
    y_size = len(chosen)
    per_y = EXPERTS // y_size
    count = gathered.shape[0]
    width = gathered.shape[1] - LANES
    slots = chosen[0].shape[0]
    turn = lax.broadcasted_iota(jnp.int32, (8, LANES), 0)
    lane = lax.broadcasted_iota(jnp.int32, (8, LANES), 1)
    to = (lax.axis_index("y") + turn) % y_size
    expert = to * per_y + lax.axis_index("z") * per_y // lax.axis_size("z")
    column = jnp.where((lane == expert) & (turn < y_size), 1.0, 0.0).astype(jnp.bfloat16)
    share = lax.dot_general(
        column,
        gathered[:, width:],
        (((1,), (1,)), ((), ())),
        preferred_element_type=jnp.float32,
    )
    named = share > 0
    first = lax.broadcasted_iota(jnp.int32, (count, count), 0)
    second = lax.broadcasted_iota(jnp.int32, (count, count), 1)
    earlier = (first < second) & (first // row_count == second // row_count)
    slot = jnp.dot(
        jnp.where(named, 1.0, 0.0).astype(jnp.bfloat16),
        jnp.where(earlier, 1.0, 0.0).astype(jnp.bfloat16),
        preferred_element_type=jnp.float32,
    ).astype(jnp.int32)
    source = lax.broadcasted_iota(jnp.int32, (8, count), 1)
    target = jnp.where(named, source // row_count * MOST + slot, -1)
    place = lax.broadcasted_iota(jnp.int32, (slots, count), 0)
    for k in (2, 1, 3, 0):
        placed = place == target[k : k + 1, :]
        pick = jnp.where(placed, 1.0, 0.0).astype(jnp.bfloat16)
        chosen[k][...] = jnp.dot(
            pick, gathered[:, :width], preferred_element_type=jnp.float32
        ).astype(jnp.bfloat16)
        weigh[k] = jnp.where(placed, share[k : k + 1, :], 0.0).astype(jnp.bfloat16)


def shifted(value, axis, step):
    size = lax.axis_size(axis)
    return lax.ppermute(value, axis, [(i, (i + step) % size) for i in range(size)])


def expert_body(rows, gate_a, up_a, down_a, gate_b, up_b, down_b, out):
    value = rows[...]

    def hidden(gate, up):
        gate_act = jnp.dot(value, gate[...], preferred_element_type=jnp.float32)
        up_act = jnp.dot(value, up[...], preferred_element_type=jnp.float32)
        return (gate_act / (1.0 + jnp.exp(-gate_act)) * up_act).astype(jnp.bfloat16)

    total = jnp.dot(hidden(gate_a, up_a), down_a[...], preferred_element_type=jnp.float32)
    total += jnp.dot(hidden(gate_b, up_b), down_b[...], preferred_element_type=jnp.float32)
    out[...] = total.astype(jnp.bfloat16)


def expert_part(rows, weights):
    whole = pl.BlockSpec(memory_space=pltpu.VMEM)
    units = 2 * weights[0].shape[1]
    return pl.pallas_call(
        expert_body,
        out_shape=jax.ShapeDtypeStruct(rows.shape, jnp.bfloat16),
        in_specs=[whole] * 7,
        out_specs=whole,
        cost_estimate=pl.CostEstimate(
            flops=6 * rows.shape[0] * rows.shape[1] * units,
            transcendentals=rows.shape[0] * units,
            bytes_accessed=4 * rows.size + 6 * rows.shape[1] * units,
        ),
        compiler_params=pltpu.CompilerParams(vmem_limit_bytes=16 << 20),
    )(rows, *weights)


def layer(
    hidden_states,
    norm_gain,
    expert_ids,
    route_scores,
    gate_weight,
    up_weight,
    down_weight,
    query_latent,
    query_rope,
    cache_latent,
    cache_rope,
    tree_latent,
    tree_rope,
    cache_lengths,
    tree_parents,
):
    row_count, width = hidden_states.shape
    whole = pl.BlockSpec(memory_space=pltpu.VMEM)
    packed = pl.pallas_call(
        pack_body,
        out_shape=jax.ShapeDtypeStruct((row_count, width + LANES), jnp.bfloat16),
        in_specs=[whole] * 4,
        out_specs=whole,
    )(hidden_states, norm_gain[None, :], expert_ids, route_scores)
    gathered = lax.all_gather(packed, "z", axis=0, tiled=True)

    y_size = lax.axis_size("y")
    slots = gathered.shape[0] // row_count * MOST
    part = jax.ShapeDtypeStruct((slots, width), jnp.bfloat16)
    *chosen, weigh = pl.pallas_call(
        functools.partial(select_body, row_count),
        out_shape=[part] * y_size
        + [jax.ShapeDtypeStruct((y_size, slots, gathered.shape[0]), jnp.bfloat16)],
        in_specs=[whole],
        out_specs=[whole] * (y_size + 1),
    )(gathered)
    *chosen, gate_weight, up_weight, down_weight = lax.optimization_barrier(
        (*chosen, gate_weight, up_weight, down_weight)
    )
    own = (gate_weight, up_weight, down_weight)
    weights = own + tuple(shifted(w, "c", 1) for w in own)

    arrived = [chosen[0]]
    for k in range(1, y_size):
        arrived.append(shifted(chosen[k], "y", k))
    returned = []
    for k in range(y_size):
        answer = expert_part(arrived[k], weights)
        returned.append(shifted(answer, "y", -k) if k else answer)

    attention_out = attend_request(
        query_latent,
        query_rope,
        cache_latent[0],
        cache_rope[0],
        tree_latent,
        tree_rope,
        cache_lengths[0],
        tree_parents,
    )

    summed = sum(
        lax.dot_general(
            weigh[k], returned[k], (((0,), (0,)), ((), ())), preferred_element_type=jnp.float32
        )
        for k in range(y_size)
    ).astype(jnp.bfloat16)
    parts = lax.all_to_all(summed, "z", split_axis=0, concat_axis=0, tiled=True)
    expert_out = jnp.sum(parts.reshape(-1, row_count, width).astype(jnp.float32), axis=0)
    return (attention_out, expert_out.astype(jnp.bfloat16))


def solution(mesh):
    devices = mesh.devices.reshape(4, 4, 16, 2)
    grid = Mesh(devices, grid_axes)
    rows = P(grid_axes, None)
    ep = ("y", "z", "c")
    placed = (
        rows,
        P(),
        rows,
        rows,
        P(None, ep),
        P(None, ep),
        P(ep, None),
        P(grid_axes, None, None),
        rows,
        P(grid_axes, None, None),
        P(grid_axes, None, None),
        rows,
        rows,
        P(grid_axes),
        P(grid_axes),
    )
    return jax.shard_map(
        layer,
        mesh=grid,
        in_specs=placed,
        out_specs=(P(grid_axes, None, None), rows),
        check_vma=False,
    )
```

```python
import functools

import jax
import jax.numpy as jnp
from jax import lax
from jax.experimental import pallas as pl
from jax.experimental.pallas import tpu as pltpu
from jax.sharding import Mesh, PartitionSpec as P


EXPERTS = 16
MOST = 5
LANES = 128

softmax_scale = 192.0 ** (-0.5)
route_scale = 2.5
norm_eps = 1e-06
very_negative = -1e30
grid_axes = ("dp", "y", "z", "c")


def visible_tree(parents):
    tree_size = parents.shape[0]
    position = jnp.arange(tree_size, dtype=jnp.int32)
    parent_map = ((parents[:, None] == position[None, :]) & (position[:, None] > 0)).astype(
        jnp.float32
    )
    identity = jnp.eye(tree_size, dtype=jnp.float32)
    reached = identity
    for _ in range(tree_size):
        reached = jnp.minimum(
            identity + jnp.dot(parent_map, reached, precision=lax.Precision.HIGHEST), 1.0
        )
    return reached > 0.5


def attend_request(
    query_latent,
    query_rope,
    cache_latent,
    cache_rope,
    tree_latent,
    tree_rope,
    cache_length,
    parents,
):
    row_count = query_latent.shape[0]
    head_count = query_latent.shape[1]
    rope_width = tree_rope.shape[1]
    query_rotary = query_rope.reshape(row_count, head_count, rope_width)
    cache_scores = jnp.einsum(
        "rhc,lc->rhl", query_latent, cache_latent, preferred_element_type=jnp.float32
    )
    cache_scores = (
        cache_scores
        + jnp.einsum("rhc,cl->rhl", query_rotary, cache_rope, preferred_element_type=jnp.float32)
    ) * softmax_scale
    candidate_tree_scores = jnp.einsum(
        "rhc,jc->rhj", query_latent, tree_latent, preferred_element_type=jnp.float32
    )
    candidate_tree_scores = (
        candidate_tree_scores
        + jnp.einsum("rhc,jc->rhj", query_rotary, tree_rope, preferred_element_type=jnp.float32)
    ) * softmax_scale
    cache_live = (jnp.arange(cache_latent.shape[0], dtype=jnp.int32) < cache_length)[None, None, :]
    tree_seen = visible_tree(parents)[:, None, :]
    cache_scores = jnp.where(cache_live, cache_scores, very_negative)
    candidate_tree_scores = jnp.where(tree_seen, candidate_tree_scores, very_negative)
    row_peak = jnp.maximum(
        jnp.max(cache_scores, axis=-1, keepdims=True),
        jnp.max(candidate_tree_scores, axis=-1, keepdims=True),
    )
    cache_exp = jnp.where(cache_live, jnp.exp(cache_scores - row_peak), 0.0)
    tree_exp = jnp.where(tree_seen, jnp.exp(candidate_tree_scores - row_peak), 0.0)
    denominator = jnp.sum(cache_exp, axis=-1, keepdims=True) + jnp.sum(
        tree_exp, axis=-1, keepdims=True
    )
    cache_probs = (cache_exp / denominator).astype(jnp.bfloat16)
    tree_probs = (tree_exp / denominator).astype(jnp.bfloat16)
    attended = jnp.einsum(
        "rhl,lc->rhc", cache_probs, cache_latent, preferred_element_type=jnp.float32
    )
    attended = attended + jnp.einsum(
        "rhj,jc->rhc", tree_probs, tree_latent, preferred_element_type=jnp.float32
    )
    return attended.astype(jnp.bfloat16)


def pack_body(states, gain, ids, scores, out):
    value = states[...].astype(jnp.float32)
    row_count, width = value.shape
    mean = jnp.mean(value * value, axis=-1, keepdims=True)
    out[:, :width] = (value * lax.rsqrt(mean + norm_eps) * gain[...]).astype(jnp.bfloat16)
    score = scores[...]
    weight = (route_scale * score / jnp.sum(score, axis=-1, keepdims=True)).astype(jnp.bfloat16)
    weight = weight.astype(jnp.float32)
    names = ids[...]
    lane = lax.broadcasted_iota(jnp.int32, (row_count, LANES), 1)
    table = jnp.zeros((row_count, LANES), jnp.float32)
    for k in range(names.shape[1]):
        table += jnp.where(names[:, k : k + 1] == lane, weight[:, k : k + 1], 0.0)
    out[:, width:] = table.astype(jnp.bfloat16)


def select_body(row_count, gathered, *outs):
    chosen, weigh = outs[:-1], outs[-1]
    y_size = len(chosen)
    per_y = EXPERTS // y_size
    count = gathered.shape[0]
    width = gathered.shape[1] - LANES
    slots = chosen[0].shape[0]
    turn = lax.broadcasted_iota(jnp.int32, (8, LANES), 0)
    lane = lax.broadcasted_iota(jnp.int32, (8, LANES), 1)
    to = (lax.axis_index("y") + turn) % y_size
    expert = to * per_y + lax.axis_index("z") * per_y // lax.axis_size("z")
    column = jnp.where((lane == expert) & (turn < y_size), 1.0, 0.0).astype(jnp.bfloat16)
    share = lax.dot_general(
        column,
        gathered[:, width:],
        (((1,), (1,)), ((), ())),
        preferred_element_type=jnp.float32,
    )
    named = share > 0
    first = lax.broadcasted_iota(jnp.int32, (count, count), 0)
    second = lax.broadcasted_iota(jnp.int32, (count, count), 1)
    earlier = (first < second) & (first // row_count == second // row_count)
    slot = jnp.dot(
        jnp.where(named, 1.0, 0.0).astype(jnp.bfloat16),
        jnp.where(earlier, 1.0, 0.0).astype(jnp.bfloat16),
        preferred_element_type=jnp.float32,
    ).astype(jnp.int32)
    source = lax.broadcasted_iota(jnp.int32, (8, count), 1)
    target = jnp.where(named, source // row_count * MOST + slot, -1)
    place = lax.broadcasted_iota(jnp.int32, (slots, count), 0)
    for k in (2, 1, 3, 0):
        placed = place == target[k : k + 1, :]
        pick = jnp.where(placed, 1.0, 0.0).astype(jnp.bfloat16)
        chosen[k][...] = jnp.dot(
            pick, gathered[:, :width], preferred_element_type=jnp.float32
        ).astype(jnp.bfloat16)
        weigh[k] = jnp.where(placed, share[k : k + 1, :], 0.0).astype(jnp.bfloat16)


def shifted(value, axis, step):
    size = lax.axis_size(axis)
    return lax.ppermute(value, axis, [(i, (i + step) % size) for i in range(size)])


def expert_body(count, *refs):
    rows, (gate_a, up_a, down_a, gate_b, up_b, down_b), outs = (
        refs[:count],
        refs[count : count + 6],
        refs[count + 6 :],
    )
    value = jnp.concatenate([row[...] for row in rows], axis=0)

    def hidden(gate, up):
        gate_act = jnp.dot(value, gate[...], preferred_element_type=jnp.float32)
        up_act = jnp.dot(value, up[...], preferred_element_type=jnp.float32)
        return (gate_act / (1.0 + jnp.exp(-gate_act)) * up_act).astype(jnp.bfloat16)

    total = jnp.dot(hidden(gate_a, up_a), down_a[...], preferred_element_type=jnp.float32)
    total += jnp.dot(hidden(gate_b, up_b), down_b[...], preferred_element_type=jnp.float32)
    size = rows[0].shape[0]
    for k, out in enumerate(outs):
        out[...] = total[k * size : (k + 1) * size].astype(jnp.bfloat16)


def expert_part(rows, weights):
    whole = pl.BlockSpec(memory_space=pltpu.VMEM)
    units = 2 * weights[0].shape[1]
    size, width = len(rows) * rows[0].shape[0], rows[0].shape[1]
    return pl.pallas_call(
        functools.partial(expert_body, len(rows)),
        out_shape=[jax.ShapeDtypeStruct(row.shape, jnp.bfloat16) for row in rows],
        in_specs=[whole] * (len(rows) + 6),
        out_specs=[whole] * len(rows),
        cost_estimate=pl.CostEstimate(
            flops=6 * size * width * units,
            transcendentals=size * units,
            bytes_accessed=4 * size * width + 6 * width * units,
        ),
        compiler_params=pltpu.CompilerParams(vmem_limit_bytes=28 << 20),
    )(*rows, *weights)


def expand_body(weigh, *refs):
    out = refs[-1]
    total = jnp.zeros(out.shape, jnp.float32)
    for k, answer in enumerate(refs[:-1]):
        total += lax.dot_general(
            weigh[k],
            answer[...],
            (((0,), (0,)), ((), ())),
            preferred_element_type=jnp.float32,
        )
    out[...] = total.astype(jnp.bfloat16)


def layer(
    hidden_states,
    norm_gain,
    expert_ids,
    route_scores,
    gate_weight,
    up_weight,
    down_weight,
    query_latent,
    query_rope,
    cache_latent,
    cache_rope,
    tree_latent,
    tree_rope,
    cache_lengths,
    tree_parents,
):
    row_count, width = hidden_states.shape
    whole = pl.BlockSpec(memory_space=pltpu.VMEM)
    packed = pl.pallas_call(
        pack_body,
        out_shape=jax.ShapeDtypeStruct((row_count, width + LANES), jnp.bfloat16),
        in_specs=[whole] * 4,
        out_specs=whole,
    )(hidden_states, norm_gain, expert_ids, route_scores)
    gathered = lax.all_gather(packed, "z", axis=0, tiled=True)

    y_size = lax.axis_size("y")
    slots = gathered.shape[0] // row_count * MOST
    part = jax.ShapeDtypeStruct((slots, width), jnp.bfloat16)
    *chosen, weigh = pl.pallas_call(
        functools.partial(select_body, row_count),
        out_shape=[part] * y_size
        + [jax.ShapeDtypeStruct((y_size, slots, gathered.shape[0]), jnp.bfloat16)],
        in_specs=[whole],
        out_specs=[whole] * (y_size + 1),
        compiler_params=pltpu.CompilerParams(vmem_limit_bytes=16 << 20),
    )(gathered)
    *chosen, gate_weight, up_weight, down_weight = lax.optimization_barrier(
        (*chosen, gate_weight, up_weight, down_weight)
    )
    own = (gate_weight, up_weight, down_weight)
    weights = own + tuple(shifted(w, "c", 1) for w in own)

    arrived = [chosen[0]]
    for k in range(1, y_size):
        arrived.append(shifted(chosen[k], "y", k))
    answers = expert_part(arrived, weights)
    returned = [answers[0]]
    for k in range(1, y_size):
        returned.append(shifted(answers[k], "y", -k))

    attention_out = attend_request(
        query_latent,
        query_rope,
        cache_latent[0],
        cache_rope[0],
        tree_latent,
        tree_rope,
        cache_lengths[0],
        tree_parents,
    )

    summed = pl.pallas_call(
        expand_body,
        out_shape=jax.ShapeDtypeStruct((gathered.shape[0], width), jnp.bfloat16),
        in_specs=[whole] * (y_size + 1),
        out_specs=whole,
        compiler_params=pltpu.CompilerParams(vmem_limit_bytes=16 << 20),
    )(weigh, *returned)
    parts = lax.all_to_all(summed, "z", split_axis=0, concat_axis=0, tiled=True)
    expert_out = jnp.sum(parts.reshape(-1, row_count, width).astype(jnp.float32), axis=0)
    return (attention_out, expert_out.astype(jnp.bfloat16))


def solution(mesh):
    devices = mesh.devices.reshape(4, 4, 16, 2)
    grid = Mesh(devices, grid_axes)
    rows = P(grid_axes, None)
    ep = ("y", "z", "c")
    placed = (
        rows,
        P(),
        rows,
        rows,
        P(None, ep),
        P(None, ep),
        P(ep, None),
        P(grid_axes, None, None),
        rows,
        P(grid_axes, None, None),
        P(grid_axes, None, None),
        rows,
        rows,
        P(grid_axes),
        P(grid_axes),
    )
    return jax.shard_map(
        layer,
        mesh=grid,
        in_specs=placed,
        out_specs=(P(grid_axes, None, None), rows),
        check_vma=False,
    )
```

```python
import functools

import jax
import jax.numpy as jnp
from jax import lax
from jax.experimental import pallas as pl
from jax.experimental.pallas import tpu as pltpu
from jax.sharding import Mesh, PartitionSpec as P


EXPERTS = 16
MOST = 5
LANES = 128

softmax_scale = 192.0 ** (-0.5)
route_scale = 2.5
norm_eps = 1e-06
very_negative = -1e30
grid_axes = ("dp", "y", "zi", "zp", "c")
z_axes = ("zi", "zp")


def visible_tree(parents):
    tree_size = parents.shape[0]
    position = jnp.arange(tree_size, dtype=jnp.int32)
    parent_map = ((parents[:, None] == position[None, :]) & (position[:, None] > 0)).astype(
        jnp.float32
    )
    identity = jnp.eye(tree_size, dtype=jnp.float32)
    reached = identity
    for _ in range(tree_size):
        reached = jnp.minimum(
            identity + jnp.dot(parent_map, reached, precision=lax.Precision.HIGHEST), 1.0
        )
    return reached > 0.5


def attend_request(
    query_latent,
    query_rope,
    cache_latent,
    cache_rope,
    tree_latent,
    tree_rope,
    cache_length,
    parents,
):
    row_count = query_latent.shape[0]
    head_count = query_latent.shape[1]
    rope_width = tree_rope.shape[1]
    query_rotary = query_rope.reshape(row_count, head_count, rope_width)
    cache_scores = jnp.einsum(
        "rhc,lc->rhl", query_latent, cache_latent, preferred_element_type=jnp.float32
    )
    cache_scores = (
        cache_scores
        + jnp.einsum("rhc,cl->rhl", query_rotary, cache_rope, preferred_element_type=jnp.float32)
    ) * softmax_scale
    candidate_tree_scores = jnp.einsum(
        "rhc,jc->rhj", query_latent, tree_latent, preferred_element_type=jnp.float32
    )
    candidate_tree_scores = (
        candidate_tree_scores
        + jnp.einsum("rhc,jc->rhj", query_rotary, tree_rope, preferred_element_type=jnp.float32)
    ) * softmax_scale
    cache_live = (jnp.arange(cache_latent.shape[0], dtype=jnp.int32) < cache_length)[None, None, :]
    tree_seen = visible_tree(parents)[:, None, :]
    cache_scores = jnp.where(cache_live, cache_scores, very_negative)
    candidate_tree_scores = jnp.where(tree_seen, candidate_tree_scores, very_negative)
    row_peak = jnp.maximum(
        jnp.max(cache_scores, axis=-1, keepdims=True),
        jnp.max(candidate_tree_scores, axis=-1, keepdims=True),
    )
    cache_exp = jnp.where(cache_live, jnp.exp(cache_scores - row_peak), 0.0)
    tree_exp = jnp.where(tree_seen, jnp.exp(candidate_tree_scores - row_peak), 0.0)
    denominator = jnp.sum(cache_exp, axis=-1, keepdims=True) + jnp.sum(
        tree_exp, axis=-1, keepdims=True
    )
    cache_probs = (cache_exp / denominator).astype(jnp.bfloat16)
    tree_probs = (tree_exp / denominator).astype(jnp.bfloat16)
    attended = jnp.einsum(
        "rhl,lc->rhc", cache_probs, cache_latent, preferred_element_type=jnp.float32
    )
    attended = attended + jnp.einsum(
        "rhj,jc->rhc", tree_probs, tree_latent, preferred_element_type=jnp.float32
    )
    return attended.astype(jnp.bfloat16)


def pack_body(states, gain, ids, scores, out):
    value = states[...].astype(jnp.float32)
    row_count, width = value.shape
    mean = jnp.mean(value * value, axis=-1, keepdims=True)
    out[:, :width] = (value * lax.rsqrt(mean + norm_eps) * gain[...]).astype(jnp.bfloat16)
    score = scores[...]
    weight = (route_scale * score / jnp.sum(score, axis=-1, keepdims=True)).astype(jnp.bfloat16)
    weight = weight.astype(jnp.float32)
    names = ids[...]
    lane = lax.broadcasted_iota(jnp.int32, (row_count, LANES), 1)
    table = jnp.zeros((row_count, LANES), jnp.float32)
    for k in range(names.shape[1]):
        table += jnp.where(names[:, k : k + 1] == lane, weight[:, k : k + 1], 0.0)
    out[:, width:] = table.astype(jnp.bfloat16)


def select_body(row_count, gathered, *outs):
    chosen, weigh = outs[:-1], outs[-1]
    y_size = len(chosen)
    per_y = EXPERTS // y_size
    count = gathered.shape[0]
    width = gathered.shape[1] - LANES
    slots = chosen[0].shape[0]
    turn = lax.broadcasted_iota(jnp.int32, (8, LANES), 0)
    lane = lax.broadcasted_iota(jnp.int32, (8, LANES), 1)
    to = (lax.axis_index("y") + turn) % y_size
    expert = to * per_y + z_index() * per_y // z_size()
    column = jnp.where((lane == expert) & (turn < y_size), 1.0, 0.0).astype(jnp.bfloat16)
    share = lax.dot_general(
        column,
        gathered[:, width:],
        (((1,), (1,)), ((), ())),
        preferred_element_type=jnp.float32,
    )
    named = share > 0
    first = lax.broadcasted_iota(jnp.int32, (count, count), 0)
    second = lax.broadcasted_iota(jnp.int32, (count, count), 1)
    earlier = (first < second) & (first // row_count == second // row_count)
    slot = jnp.dot(
        jnp.where(named, 1.0, 0.0).astype(jnp.bfloat16),
        jnp.where(earlier, 1.0, 0.0).astype(jnp.bfloat16),
        preferred_element_type=jnp.float32,
    ).astype(jnp.int32)
    source = lax.broadcasted_iota(jnp.int32, (8, count), 1)
    target = jnp.where(named, source // row_count * MOST + slot, -1)
    place = lax.broadcasted_iota(jnp.int32, (slots, count), 0)
    for k in (2, 1, 3, 0):
        placed = place == target[k : k + 1, :]
        pick = jnp.where(placed, 1.0, 0.0).astype(jnp.bfloat16)
        chosen[k][...] = jnp.dot(
            pick, gathered[:, :width], preferred_element_type=jnp.float32
        ).astype(jnp.bfloat16)
        weigh[k] = jnp.where(placed, share[k : k + 1, :], 0.0).astype(jnp.bfloat16)


def z_index():
    return lax.axis_index("zi") * lax.axis_size("zp") + lax.axis_index("zp")


def z_size():
    return lax.axis_size("zi") * lax.axis_size("zp")


def shifted(value, axis, step):
    size = z_size() if axis == z_axes else lax.axis_size(axis)
    return lax.ppermute(value, axis, [(i, (i + step) % size) for i in range(size)])


def expert_body(count, *refs):
    rows, (gate_a, up_a, down_a, gate_b, up_b, down_b), outs = (
        refs[:count],
        refs[count : count + 6],
        refs[count + 6 :],
    )
    value = jnp.concatenate([row[...] for row in rows], axis=0)

    def hidden(gate, up):
        gate_act = jnp.dot(value, gate[...], preferred_element_type=jnp.float32)
        up_act = jnp.dot(value, up[...], preferred_element_type=jnp.float32)
        return (gate_act / (1.0 + jnp.exp(-gate_act)) * up_act).astype(jnp.bfloat16)

    total = jnp.dot(hidden(gate_a, up_a), down_a[...], preferred_element_type=jnp.float32)
    total += jnp.dot(hidden(gate_b, up_b), down_b[...], preferred_element_type=jnp.float32)
    size = rows[0].shape[0]
    for k, out in enumerate(outs):
        out[...] = total[k * size : (k + 1) * size].astype(jnp.bfloat16)


def expert_part(rows, weights):
    whole = pl.BlockSpec(memory_space=pltpu.VMEM)
    units = 2 * weights[0].shape[1]
    size, width = len(rows) * rows[0].shape[0], rows[0].shape[1]
    return pl.pallas_call(
        functools.partial(expert_body, len(rows)),
        out_shape=[jax.ShapeDtypeStruct(row.shape, jnp.bfloat16) for row in rows],
        in_specs=[whole] * (len(rows) + 6),
        out_specs=[whole] * len(rows),
        cost_estimate=pl.CostEstimate(
            flops=6 * size * width * units,
            transcendentals=size * units,
            bytes_accessed=4 * size * width + 6 * width * units,
        ),
        compiler_params=pltpu.CompilerParams(vmem_limit_bytes=28 << 20),
    )(*rows, *weights)


def expand_body(row_count, weigh, *refs):
    answers, (keep, left, right, scratch) = refs[:-4], refs[-4:]
    total = jnp.zeros(scratch.shape, jnp.float32)
    for k, answer in enumerate(answers):
        total += lax.dot_general(
            weigh[k],
            answer[...],
            (((0,), (0,)), ((), ())),
            preferred_element_type=jnp.float32,
        )
    scratch[...] = total
    half = left.shape[1]
    parity = lax.axis_index("zp")
    pair = 2 * row_count
    for i in range(keep.shape[0] // pair):
        for mine in (True, False):
            odd = parity if mine else 1 - parity
            block = jnp.concatenate(
                [
                    scratch[pl.ds(pl.multiple_of((4 * i + j + odd) * row_count, 8), row_count), :]
                    for j in (0, 2)
                ],
                axis=0,
            )
            rows = pl.ds(i * pair, pair)
            if mine:
                keep[rows, :] = block
            else:
                left[rows, :] = block[:, :half].astype(jnp.bfloat16)
                right[rows, :] = block[:, half:].astype(jnp.bfloat16)


def merge_body(keep, left, right, out):
    half = left.shape[1]
    out[:, :half] = (keep[:, :half] + left[...].astype(jnp.float32)).astype(jnp.bfloat16)
    out[:, half:] = (keep[:, half:] + right[...].astype(jnp.float32)).astype(jnp.bfloat16)


def layer(
    hidden_states,
    norm_gain,
    expert_ids,
    route_scores,
    gate_weight,
    up_weight,
    down_weight,
    query_latent,
    query_rope,
    cache_latent,
    cache_rope,
    tree_latent,
    tree_rope,
    cache_lengths,
    tree_parents,
):
    row_count, width = hidden_states.shape
    whole = pl.BlockSpec(memory_space=pltpu.VMEM)
    packed = pl.pallas_call(
        pack_body,
        out_shape=jax.ShapeDtypeStruct((row_count, width + LANES), jnp.bfloat16),
        in_specs=[whole] * 4,
        out_specs=whole,
    )(hidden_states, norm_gain, expert_ids, route_scores)
    gathered = lax.all_gather(packed, z_axes, axis=0, tiled=True)

    y_size = lax.axis_size("y")
    slots = gathered.shape[0] // row_count * MOST
    part = jax.ShapeDtypeStruct((slots, width), jnp.bfloat16)
    *chosen, weigh = pl.pallas_call(
        functools.partial(select_body, row_count),
        out_shape=[part] * y_size
        + [jax.ShapeDtypeStruct((y_size, slots, gathered.shape[0]), jnp.bfloat16)],
        in_specs=[whole],
        out_specs=[whole] * (y_size + 1),
        compiler_params=pltpu.CompilerParams(vmem_limit_bytes=16 << 20),
    )(gathered)
    *chosen, gate_weight, up_weight, down_weight = lax.optimization_barrier(
        (*chosen, gate_weight, up_weight, down_weight)
    )
    own = (gate_weight, up_weight, down_weight)
    weights = own + tuple(shifted(w, "c", 1) for w in own)

    arrived = [chosen[0]]
    for k in range(1, y_size):
        arrived.append(shifted(chosen[k], "y", k))
    answers = expert_part(arrived, weights)
    returned = [answers[0]]
    for k in range(1, y_size):
        returned.append(shifted(answers[k], "y", -k))

    attention_out = attend_request(
        query_latent,
        query_rope,
        cache_latent[0],
        cache_rope[0],
        tree_latent,
        tree_rope,
        cache_lengths[0],
        tree_parents,
    )

    held = gathered.shape[0] // 2
    small = pltpu.CompilerParams(vmem_limit_bytes=16 << 20)
    keep, left, right = pl.pallas_call(
        functools.partial(expand_body, row_count),
        out_shape=[
            jax.ShapeDtypeStruct((held, width), jnp.float32),
            jax.ShapeDtypeStruct((held, width // 2), jnp.bfloat16),
            jax.ShapeDtypeStruct((held, width // 2), jnp.bfloat16),
        ],
        in_specs=[whole] * (y_size + 1),
        out_specs=[whole] * 3,
        scratch_shapes=[pltpu.VMEM((2 * held, width), jnp.float32)],
        compiler_params=small,
    )(weigh, *returned)
    left = shifted(left, z_axes, 1)
    right = shifted(right, z_axes, -1)
    merged = pl.pallas_call(
        merge_body,
        out_shape=jax.ShapeDtypeStruct((held, width), jnp.bfloat16),
        in_specs=[whole] * 3,
        out_specs=whole,
        compiler_params=small,
    )(keep, left, right)
    parts = lax.all_to_all(merged, "zi", split_axis=0, concat_axis=0, tiled=True)
    expert_out = jnp.sum(parts.reshape(-1, row_count, width).astype(jnp.float32), axis=0)
    return (attention_out, expert_out.astype(jnp.bfloat16))


def solution(mesh):
    devices = mesh.devices.reshape(4, 4, 8, 2, 2)
    grid = Mesh(devices, grid_axes)
    rows = P(grid_axes, None)
    ep = ("y", *z_axes, "c")
    placed = (
        rows,
        P(),
        rows,
        rows,
        P(None, ep),
        P(None, ep),
        P(ep, None),
        P(grid_axes, None, None),
        rows,
        P(grid_axes, None, None),
        P(grid_axes, None, None),
        rows,
        rows,
        P(grid_axes),
        P(grid_axes),
    )
    return jax.shard_map(
        layer,
        mesh=grid,
        in_specs=placed,
        out_specs=(P(grid_axes, None, None), rows),
        check_vma=False,
    )
```
